32 devices in a mesh: pages: 8 (over y, x, core), heads: 4 (over z).
Axes of the slice: x: 2, y: 2, z: 4, core: 2. Of those that a mesh axis runs over, the one named last changes fastest.
Arguments:
- hidden: bfloat16 [16, 608, 768], P('pages', 'heads'), may hold values from -6 to 6
- qkv_weight: bfloat16 [768, 3, 768], P(None, None, 'heads'), may hold values from -0.21875 to 0.21875
- qv_bias: bfloat16 [2, 768], P(None, 'heads'), may hold values from -3 to 3
- out_weight: bfloat16 [768, 768], P('heads'), may hold values from -0.875 to 0.875
- out_bias: bfloat16 [768], replicated, may hold values from -2 to 2
- first_gain: bfloat16 [768], replicated, may hold values from 0.5 to 1.5
- first_shift: bfloat16 [768], replicated, may hold values from -2 to 2
- up_weight: bfloat16 [768, 3072], P(None, 'heads'), may hold values from -0.21875 to 0.21875
- up_bias: bfloat16 [3072], P('heads'), may hold values from -2 to 2
- down_weight: bfloat16 [3072, 768], P('heads'), may hold values from -0.15625 to 0.15625
- down_bias: bfloat16 [768], replicated, may hold values from -2 to 2
- second_gain: bfloat16 [768], replicated, may hold values from 0.5 to 1.5
- second_shift: bfloat16 [768], replicated, may hold values from -2 to 2
- relative_table: bfloat16 [32, 12], P(None, 'heads'), may hold values from -4 to 4
- horizontal_table: bfloat16 [64, 12], P(None, 'heads'), may hold values from -4 to 4
- vertical_table: bfloat16 [64, 12], P(None, 'heads'), may hold values from -4 to 4
- token_mask: int32 [16, 608], P('pages'), may hold values from 0 to 1, as said below
- relative_ids: int32 [16, 608, 608], P('pages'), may hold values from 0 to 31
- horizontal_ids: int32 [16, 608, 608], P('pages'), may hold values from 0 to 63
- vertical_ids: int32 [16, 608, 608], P('pages'), may hold values from 0 to 63
- cotangent: bfloat16 [16, 608, 768], P('pages', 'heads'), may hold values from -18 to 18
Outputs:
- output: bfloat16 [16, 608, 768], P('pages', 'heads')
- grad_hidden: bfloat16 [16, 608, 768], P('pages', 'heads')
- grad_qkv_weight: float32 [768, 3, 768], P(None, None, 'heads')
- grad_qv_bias: float32 [2, 768], P(None, 'heads')
- grad_out_weight: float32 [768, 768], P('heads')
- grad_out_bias: float32 [768], replicated
- grad_first_gain: float32 [768], replicated
- grad_first_shift: float32 [768], replicated
- grad_up_weight: float32 [768, 3072], P(None, 'heads')
- grad_up_bias: float32 [3072], P('heads')
- grad_down_weight: float32 [3072, 768], P('heads')
- grad_down_bias: float32 [768], replicated
- grad_second_gain: float32 [768], replicated
- grad_second_shift: float32 [768], replicated
- grad_relative_table: float32 [32, 12], P(None, 'heads')
- grad_horizontal_table: float32 [64, 12], P(None, 'heads')
- grad_vertical_table: float32 [64, 12], P(None, 'heads')
The draws below stay inside these ranges and needn't reach their ends.
Inputs may be any that keep to these rules, and one draw needn't show every extreme that they name: `token_mask`: ones mark real tokens: in each page the text tokens fill positions 0 to L - 1, with L from 40 to 512, and the visual tokens positions 512 to 560; every draw has a page with L = 512 and one with L = 40.
All inputs are finite; a program needn't handle non-finite values.
Results may differ from the reference program's by a relative error of at most 0.02.
Values may be sent and summed in bfloat16 or wider, within the bound.
A program may use at most 192 MiB of HBM per device.

```python
import jax
import jax.numpy as jnp
from jax import lax

D = 768
HEADS = 12
HEAD_DIM = 64
FF = 3072
REL_B = 32
POS_B = 64
SEQ = 608
TEXT = 512
VIS = 49
MIN_TEXT = 40
PAGES = 16


def draw_token_mask(key, part):
    length_key = jax.random.fold_in(key, 11)
    lengths = jax.random.randint(length_key, (PAGES,), MIN_TEXT, TEXT + 1)
    lengths = lengths.at[0].set(TEXT).at[PAGES - 1].set(MIN_TEXT)
    position = jnp.arange(SEQ, dtype=jnp.int32)[None, :]
    textual = position < lengths[:, None]
    visual = (position >= TEXT) & (position < TEXT + VIS)
    return (textual | visual).astype(jnp.int32)


def draw_cotangent(key, part):
    noise_key = jax.random.fold_in(key, 21)
    ramp = 1.0 + 2.0 * jnp.arange(PAGES, dtype=jnp.float32) / (PAGES - 1)
    noise = jnp.clip(jax.random.normal(noise_key, (PAGES, SEQ, D), jnp.float32), -6.0, 6.0)
    return (noise * ramp[:, None, None]).astype(jnp.bfloat16)


def with_ends(entries, key, low, top_value):
    longest = entries.shape.index(max(entries.shape))
    spots = []
    for shift in (0, 1):
        where = [jax.random.randint(jax.random.fold_in(key, axis), (), 0, length) for axis, length in enumerate(entries.shape)]
        where[longest] = (where[longest] + shift) % entries.shape[longest]
        spots.append(tuple(where))
    return entries.at[spots[0]].set(low).at[spots[1]].set(top_value)


def block_scale(rng, dims, split, smallest, largest):
    def one(dim, parts):
        steps = jax.random.uniform(jax.random.fold_in(jax.random.fold_in(rng, 6), dim), (parts,), jnp.float32, smallest / len(split), largest / len(split))
        return jnp.repeat(jnp.exp(steps), dims[dim] // parts).reshape((-1,) + (1,) * (len(dims) - dim - 1))

    factor_of = one(*split[0])
    for cut in split[1:]:
        factor_of = factor_of * one(*cut)
    return factor_of


def normal_values(own_key, dims, width, reach, split=(), kind=jnp.bfloat16):
    entries = width * jax.random.normal(own_key, dims, jnp.float32)
    if split:
        entries = entries * block_scale(own_key, dims, split, -0.22, 0.18)
    return jnp.clip(entries, -reach, reach).astype(kind)


def setup_inputs(seed: int = 0) -> dict:
    seeds = jax.random.split(jax.random.key(seed), 22)
    hidden = normal_values(seeds[0], (PAGES, SEQ, D), 1.0, 6.0, ((0, 8), (1, 4)))
    qkv_weight = normal_values(seeds[1], (D, 3, D), D ** -0.5, 0.21875, ((2, 4),))
    qv_bias = normal_values(seeds[2], (2, D), 0.5, 3.0, ((1, 4),))
    out_weight = normal_values(seeds[3], (D, D), (D // 16) ** -0.5, 0.875, ((0, 4),))
    out_bias = normal_values(seeds[4], (D,), 0.3, 2.0)
    first_gain = jnp.clip(1.0 + 0.1 * jax.random.normal(seeds[5], (D,), jnp.float32), 0.5, 1.5).astype(jnp.bfloat16)
    first_shift = normal_values(seeds[6], (D,), 0.3, 2.0)
    up_weight = normal_values(seeds[7], (D, FF), D ** -0.5, 0.21875, ((1, 4),))
    up_bias = normal_values(seeds[8], (FF,), 0.3, 2.0, ((0, 4),))
    down_weight = normal_values(seeds[9], (FF, D), (FF // 2) ** -0.5, 0.15625, ((0, 4),))
    down_bias = normal_values(seeds[10], (D,), 0.3, 2.0)
    second_gain = jnp.clip(1.0 + 0.1 * jax.random.normal(seeds[11], (D,), jnp.float32), 0.5, 1.5).astype(jnp.bfloat16)
    second_shift = normal_values(seeds[12], (D,), 0.3, 2.0)
    relative_table = normal_values(seeds[13], (REL_B, HEADS), 1.0, 4.0, ((1, 4),))
    horizontal_table = normal_values(seeds[14], (POS_B, HEADS), 1.0, 4.0, ((1, 4),))
    vertical_table = normal_values(seeds[15], (POS_B, HEADS), 1.0, 4.0, ((1, 4),))
    token_mask = draw_token_mask(jax.random.fold_in(seeds[21], 71), 0)
    relative_ids = with_ends(jax.random.randint(seeds[17], (PAGES, SEQ, SEQ), 0, REL_B), jax.random.fold_in(seeds[17], 1), 0, REL_B - 1).astype(jnp.int32)
    horizontal_ids = with_ends(jax.random.randint(seeds[18], (PAGES, SEQ, SEQ), 0, POS_B), jax.random.fold_in(seeds[18], 1), 0, POS_B - 1).astype(jnp.int32)
    vertical_ids = with_ends(jax.random.randint(seeds[19], (PAGES, SEQ, SEQ), 0, POS_B), jax.random.fold_in(seeds[19], 1), 0, POS_B - 1).astype(jnp.int32)
    cotangent = draw_cotangent(jax.random.fold_in(seeds[21], 71), 0)
    return {"hidden": hidden, "qkv_weight": qkv_weight, "qv_bias": qv_bias, "out_weight": out_weight, "out_bias": out_bias, "first_gain": first_gain, "first_shift": first_shift, "up_weight": up_weight, "up_bias": up_bias, "down_weight": down_weight, "down_bias": down_bias, "second_gain": second_gain, "second_shift": second_shift, "relative_table": relative_table, "horizontal_table": horizontal_table, "vertical_table": vertical_table, "token_mask": token_mask, "relative_ids": relative_ids, "horizontal_ids": horizontal_ids, "vertical_ids": vertical_ids, "cotangent": cotangent}


@jax.custom_vjp
def low(v):
    return lax.optimization_barrier(v.astype(jnp.bfloat16)).astype(jnp.float32)

@jax.custom_vjp
def low_back(v):
    return v

def low_keep(v):
    return (low(v), None)

def low_pass(kept, grad):
    return (grad,)

def back_keep(v):
    return (v, None)

def back_low(kept, grad):
    return (low(grad),)
low.defvjp(low_keep, low_pass)
low_back.defvjp(back_keep, back_low)

def norm_rows(value, gain, shift):
    middle = lax.optimization_barrier(jnp.mean(value, axis=-1, keepdims=True))
    centred = value - middle
    spread = lax.optimization_barrier(jnp.mean(centred * centred, axis=-1, keepdims=True))
    return centred * lax.rsqrt(spread + 1e-12) * gain + shift

def product(form, left, right):
    return jnp.einsum(form, left, right, precision=lax.Precision.HIGHEST)

def page_block(params, block):
    qkv_weight, qv_bias, out_weight, out_bias, first_gain, first_shift, up_weight, up_bias, down_weight, down_bias, second_gain, second_shift, relative_table, horizontal_table, vertical_table = params
    hidden, mask_block, relative_ids, horizontal_ids, vertical_ids = block
    pages_in = hidden.shape[0]
    projected = product('gsd,dke->gske', hidden, qkv_weight)
    zero_row = jnp.zeros_like(qv_bias[0])
    projected = projected + jnp.stack([qv_bias[0], zero_row, qv_bias[1]])
    projected = low(low_back(projected))
    queries = projected[:, :, 0].reshape(pages_in, SEQ, HEADS, HEAD_DIM)
    keys_all = projected[:, :, 1].reshape(pages_in, SEQ, HEADS, HEAD_DIM)
    values_all = projected[:, :, 2].reshape(pages_in, SEQ, HEADS, HEAD_DIM)
    scores = product('gqhd,gkhd->ghqk', queries, keys_all) * 0.125
    table_bias = relative_table[relative_ids] + horizontal_table[horizontal_ids] + vertical_table[vertical_ids]
    scores = scores + jnp.transpose(table_bias, (0, 3, 1, 2))
    scores = low_back(scores)
    scores = jnp.where(mask_block[:, None, None, :] > 0, scores, -1000000000.0)
    row_max = lax.optimization_barrier(jnp.max(scores, axis=-1, keepdims=True))
    weights = jnp.exp(scores - row_max)
    attention = weights / lax.optimization_barrier(jnp.sum(weights, axis=-1, keepdims=True))
    attention = low(attention)
    attended = product('ghqk,gkhd->gqhd', attention, values_all).reshape(pages_in, SEQ, D)
    attended = low(low_back(attended))
    branch = low_back(product('gsc,cd->gsd', attended, out_weight) + out_bias)
    first_norm = norm_rows(hidden + branch, first_gain, first_shift)
    pre_act = low_back(product('gsd,df->gsf', low(first_norm), up_weight) + up_bias)
    activated = low(jax.nn.gelu(pre_act, approximate=False))
    ffn_out = low_back(product('gsf,fd->gsd', activated, down_weight) + down_bias)
    return norm_rows(first_norm + ffn_out, second_gain, second_shift)

def forward(hidden, params, token_mask, relative_ids, horizontal_ids, vertical_ids):
    group_count = hidden.shape[0] // 4

    def to_groups(array):
        return array.reshape((group_count, 4) + array.shape[1:])
    blocks = (to_groups(hidden), to_groups(token_mask), to_groups(relative_ids), to_groups(horizontal_ids), to_groups(vertical_ids))
    checked = jax.checkpoint(page_block)
    result = lax.map(lambda block: checked(params, block), blocks)
    return result.reshape(hidden.shape)

def reference(hidden, qkv_weight, qv_bias, out_weight, out_bias, first_gain, first_shift, up_weight, up_bias, down_weight, down_bias, second_gain, second_shift, relative_table, horizontal_table, vertical_table, token_mask, relative_ids, horizontal_ids, vertical_ids, cotangent):
    params = tuple((item.astype(jnp.float32) for item in (qkv_weight, qv_bias, out_weight, out_bias, first_gain, first_shift, up_weight, up_bias, down_weight, down_bias, second_gain, second_shift, relative_table, horizontal_table, vertical_table)))
    hidden_f = hidden.astype(jnp.float32)

    def layer(inputs, weights):
        return forward(inputs, weights, token_mask, relative_ids, horizontal_ids, vertical_ids)
    result, pullback = jax.vjp(layer, hidden_f, params)
    grad_input, grads = pullback(cotangent.astype(jnp.float32))
    return (result.astype(jnp.bfloat16), grad_input.astype(jnp.bfloat16), grads[0], grads[1], grads[2], grads[3], grads[4], grads[5], grads[6], grads[7], grads[8], grads[9], grads[10], grads[11], grads[12], grads[13], grads[14])
```

```python
import jax
import jax.numpy as jnp
from jax import lax
from jax.experimental import pallas as pl
from jax.experimental.pallas import tpu as pltpu
from jax.sharding import PartitionSpec as P
bf=jnp.bfloat16; f32=jnp.float32

def nn(a,b): return lax.dot_general(a,b,(((1,),(0,)),((),())),preferred_element_type=f32)
def nt(a,b): return lax.dot_general(a,b,(((1,),(1,)),((),())),preferred_element_type=f32)
def tn(a,b): return lax.dot_general(a,b,(((0,),(0,)),((),())),preferred_element_type=f32)

def ln_stats(v):
    mu=jnp.mean(v,axis=-1,keepdims=True)
    c=v-mu
    r=lax.rsqrt(jnp.mean(c*c,axis=-1,keepdims=True)+1e-12)
    return c*r,r

class Cfg: pass

def compute_kernel(c, koff_fn, xf, ct, i1, i2, i3, mask, wa, wu, wd, qvb, ub, tab, vec,
                   out_o, dh_o, ga_h, gu_h, gd_h, sm_o, tg_o,
                   wav, wuv, wdv, wsem, gsem, bias, PR, QT, KT, VT, att, fn, n1, r1s, act, gp, dsb, dOT, acc, dQ, dKV, flow, dffn, dsec):
    R=c.R; S=c.S; Z=c.Z; H=c.H; HD=c.HD; D=c.D; SP=c.SP; L=H*HD
    koff=koff_fn()
    cps=[pltpu.make_async_copy(a,b,wsem.at[j]) for j,(a,b) in enumerate(((wa,wav),(wu,wuv),(wd,wdv)))]
    for cp in cps: cp.start()
    wa,wu,wd=wav,wuv,wdv
    gcp=[]
    ga_o,gu_o,gd_o=wa,wu,wd
    own=lambda: xf[pl.ds(koff,R),:]
    nl=SP//128
    def bias_body(q,_):
        i=pl.multiple_of(q*8,8)
        for l in range(nl):
            w=min(128,S-l*128)
            sl=pl.ds(l*128,w)
            idx=[]
            for r in (i1,i2,i3):
                v=r[pl.ds(i,8),sl]
                if w<128: v=jnp.concatenate([v,jnp.zeros((8,128-w),jnp.int32)],axis=1)
                idx.append(v)
            for h in range(Z*H):
                g=None
                for t in range(3):
                    row=jnp.broadcast_to(tab[t,h:h+1,:],(8,128))
                    x=jnp.take_along_axis(row,idx[t],axis=1,mode="promise_in_bounds")
                    g=x if g is None else g+x
                bias[h,pl.ds(i,8),pl.ds(l*128,128)]=g
        return 0
    lax.fori_loop(0,R//8,bias_body,0)
    cps[0].wait()
    def qkv_body(z,_):
        bcol=jnp.transpose(qvb[z])
        q=nt(wa[z,0:L,:],own())+bcol[0:L,0:1]
        QT[z]=q.astype(bf)*jnp.bfloat16(0.125)
        KT[z]=nt(wa[z,L:2*L,:],xf[...]).astype(bf)
        VT[z]=(nt(wa[z,2*L:3*L,:],xf[...])+bcol[L:2*L,0:1]).astype(bf)
        return 0
    lax.fori_loop(0,Z,qkv_body,0)
    CH=16
    def fwd_body(z,_):
        outs=[]
        for hl in range(H):
            h=z*H+hl
            rs=slice(hl*HD,(hl+1)*HD)
            bias[h]=bias[h]+tn(QT[z,rs,:],KT[z,rs,:])
            def chunk(q,_):
                i=pl.multiple_of(q*CH,CH)
                s=bias[h,pl.ds(i,CH),:]
                s=jnp.where(mask[0:1,:]>0,s,-1e9)
                m=jnp.max(s,axis=-1,keepdims=True)
                e=jnp.exp(s-m)
                p=e*(1.0/jnp.sum(e,axis=-1,keepdims=True))
                PR[h,pl.ds(i,CH),:]=p.astype(bf)
                return 0
            lax.fori_loop(0,R//CH,chunk,0,unroll=True)
            outs.append(nt(PR[h],VT[z,rs,:]).astype(bf))
        att[z]=jnp.concatenate(outs,axis=1)
        return 0
    lax.fori_loop(0,Z,fwd_body,0)
    acc[...]=own().astype(f32)+vec[0:1,:]
    def out_body(z,_):
        acc[...]+=nn(att[z],wa[z,3*L:4*L,:])
        return 0
    lax.fori_loop(0,Z,out_body,0)
    def ln1(q,_):
        i=pl.multiple_of(q*CH,CH); s=pl.ds(i,CH)
        n,r=ln_stats(acc[s,:])
        n1[s,:]=n; r1s[s,:]=jnp.broadcast_to(r,(CH,128))
        f=n*vec[1:2,:]+vec[2:3,:]
        fn[s,:]=f; flow[s,:]=f.astype(bf)
        return 0
    lax.fori_loop(0,R//CH,ln1,0,unroll=True)
    cps[1].wait(); cps[2].wait()
    acc[...]=fn[...]+vec[3:4,:]
    FZ=c.FZ
    def ffn_body(z,_):
        for n0 in range(0,FZ,256):
            ns=slice(n0,n0+256)
            pre=nn(flow[...],wu[z,:,ns])+ub[z,0:1,ns]
            phi=0.5*(1.0+lax.erf(pre*0.7071067811865476))
            act[z,:,ns]=(pre*phi).astype(bf)
            gp[z,:,ns]=(phi+pre*(0.3989422804014327*jnp.exp(-0.5*pre*pre))).astype(bf)
        acc[...]+=nn(act[z],wd[z])
        return 0
    lax.fori_loop(0,Z,ffn_body,0)
    zero=jnp.zeros((8,D),f32)
    def rsum(x): return jnp.sum(x.reshape(x.shape[0]//8,8,D),axis=0)
    def ln2(q,car):
        a,b,d=car
        i=pl.multiple_of(q*CH,CH); s=pl.ds(i,CH)
        n,r=ln_stats(acc[s,:])
        out_o[s,:]=(n*vec[4:5,:]+vec[5:6,:]).astype(bf)
        g=ct[s,:].astype(f32)
        gg=g*vec[4:5,:]
        ds=r*(gg-jnp.mean(gg,axis=-1,keepdims=True)-n*jnp.mean(gg*n,axis=-1,keepdims=True))
        dsec[s,:]=ds
        lo=ds.astype(bf); dffn[s,:]=lo
        return (a+rsum(g*n),b+rsum(g),d+rsum(lo.astype(f32)))
    a,b,d=lax.fori_loop(0,R//CH,ln2,(zero,zero,zero),unroll=True)
    sm_o[4:5,:]=jnp.sum(a,axis=0,keepdims=True); sm_o[5:6,:]=jnp.sum(b,axis=0,keepdims=True); sm_o[3:4,:]=jnp.sum(d,axis=0,keepdims=True)
    def ffb_body(z,_):
        dp=(nt(dffn[...],wd[z])*gp[z].astype(f32)).astype(bf)
        gd_o[z]=tn(act[z],dffn[...]).astype(bf)
        act[z]=dp
        sm_o[pl.ds(8+z*8,8),:]=nn(jnp.ones((8,R),bf),dp)
        dsec[...]+=nt(dp,wu[z])
        gu_o[z]=tn(flow[...],dp).astype(bf)
        return 0
    lax.fori_loop(0,Z,ffb_body,0)
    def ln1b(q,car):
        a,b,d=car
        i=pl.multiple_of(q*CH,CH); s=pl.ds(i,CH)
        n=n1[s,:]; r=r1s[s,0:1]; g=dsec[s,:]
        gg=g*vec[1:2,:]
        ds=r*(gg-jnp.mean(gg,axis=-1,keepdims=True)-n*jnp.mean(gg*n,axis=-1,keepdims=True))
        fn[s,:]=ds
        lo=ds.astype(bf); dffn[s,:]=lo
        return (a+rsum(g*n),b+rsum(g),d+rsum(lo.astype(f32)))
    a,b,d=lax.fori_loop(0,R//CH,ln1b,(zero,zero,zero),unroll=True)
    sm_o[1:2,:]=jnp.sum(a,axis=0,keepdims=True); sm_o[2:3,:]=jnp.sum(b,axis=0,keepdims=True); sm_o[0:1,:]=jnp.sum(d,axis=0,keepdims=True)
    dh_o[...]=jnp.zeros(dh_o.shape,f32)
    dh_o[pl.ds(koff,R),:]=fn[...]
    def bwd_body(z,_):
        dOT[...]=nt(wa[z,3*L:4*L,:],dffn[...]).astype(bf)
        ga_o[z,3*L:4*L,:]=tn(att[z],dffn[...]).astype(bf)
        for hl in range(H):
            h=z*H+hl
            rs=slice(hl*HD,(hl+1)*HD)
            bias[h]=tn(dOT[rs,:],VT[z,rs,:])
            def chunk(q,_):
                i=pl.multiple_of(q*CH,CH); s=pl.ds(i,CH)
                p=PR[h,s,:].astype(f32); dp=bias[h,s,:]
                inner=jnp.sum(p*dp,axis=-1,keepdims=True)
                ds=p*(dp-inner)
                bias[h,s,:]=ds
                dsb[s,:]=ds.astype(bf)
                return 0
            lax.fori_loop(0,R//CH,chunk,0,unroll=True)
            dQ[rs,:]=(nt(KT[z,rs,:],dsb[...])*0.125).astype(bf)
            dKV[hl*HD:(hl+1)*HD,:]=nn(QT[z,rs,:],dsb[...]).astype(bf)
            dKV[L+hl*HD:L+(hl+1)*HD,:]=nn(dOT[rs,:],PR[h]).astype(bf)
        sm_o[pl.ds(40+z*8,8),0:L]=nt(jnp.ones((8,R),bf),dQ[...])
        sm_o[pl.ds(72+z*8,8),0:L]=nt(jnp.ones((8,SP),bf),dKV[L:2*L,:])
        dh_o[pl.ds(koff,R),:]+=tn(dQ[...],wa[z,0:L,:])
        dh_o[...]+=tn(dKV[...],wa[z,L:3*L,:])
        ga_o[z,0:L,:]=nn(dQ[...],own()).astype(bf)
        ga_o[z,L:3*L,:]=nn(dKV[...],xf[...]).astype(bf)
        return 0
    lax.fori_loop(0,Z,bwd_body,0)
    for j,(a,b) in enumerate(((wa,ga_h),(wu,gu_h),(wd,gd_h))):
        gcp.append(pltpu.make_async_copy(a,b,gsem.at[j])); gcp[-1].start()
    tg_o[...]=jnp.zeros(tg_o.shape,f32)
    HH=Z*H
    dsf=bias.reshape(HH*R,SP) if False else bias
    U=16
    it=lax.broadcasted_iota(jnp.int32,(16,S),0).astype(jnp.int16)
    one=jnp.bfloat16(1); nil=jnp.bfloat16(0)
    def hist(q,_):
        hot=[]; grads=[]
        for u in range(U):
            i=q*U+u
            rows=bias[:,pl.ds(i,1),:].reshape(HH,SP)
            grads.append(jnp.concatenate([rows,jnp.zeros((16-HH,SP),f32)],axis=0).astype(bf)[:,:S])
            parts=[]
            for r,nb in ((i1,c.B1),(i2,c.B2),(i3,c.B2)):
                row=jnp.broadcast_to(r[pl.ds(i,1),:],(16,S)).astype(jnp.int16)
                for k in range(nb//16):
                    parts.append(jnp.where(row==it+jnp.int16(16*k),one,nil))
            hot.append(jnp.concatenate(parts,axis=0))
        tot=None
        for u in range(U):
            x=nt(grads[u],hot[u])
            tot=x if tot is None else tot+x
        tg_o[...]+=tot
        return 0
    lax.fori_loop(0,R//U,hist,0)
    for g in gcp: g.wait()

def scratch(c):
    R,SP,Z,H,HD,D,FZ=c.R,c.SP,c.Z,c.H,c.HD,c.D,c.FZ
    L=H*HD
    V=pltpu.VMEM
    return [V((Z,4*L,D),bf),V((Z,D,FZ),bf),V((Z,FZ,D),bf),pltpu.SemaphoreType.DMA((3,)),pltpu.SemaphoreType.DMA((3,)),V((Z*H,R,SP),f32),V((Z*H,R,SP),bf),V((Z,L,R),bf),V((Z,L,SP),bf),V((Z,L,SP),bf),V((Z,R,L),bf),
            V((R,D),f32),V((R,D),f32),V((R,128),f32),V((Z,R,FZ),bf),V((Z,R,FZ),bf),V((R,SP),bf),V((L,R),bf),V((R,D),f32),
            V((L,R),bf),V((2*L,SP),bf),V((R,D),bf),V((R,D),bf),V((R,D),f32)]
def outs(c):
    R,SP,Z,H,HD,D,FZ=c.R,c.SP,c.Z,c.H,c.HD,c.D,c.FZ
    L=H*HD; sd=jax.ShapeDtypeStruct
    return [sd((R,D),bf),sd((SP,D),f32),sd((Z,4*L,D),bf),sd((Z,D,FZ),bf),sd((Z,FZ,D),bf),sd((104,D),f32),sd((16,c.B1+2*c.B2),f32)]

def specs():
    v=pl.BlockSpec(memory_space=pltpu.VMEM); a=pl.BlockSpec(memory_space=pl.ANY)
    return [v]*6+[a]*3+[v]*4,[v,v,a,a,a,v,v]


def shards(hidden, qkv_weight, qv_bias, out_weight, out_bias, first_gain, first_shift, up_weight, up_bias,
           down_weight, down_bias, second_gain, second_shift, relative_table, horizontal_table, vertical_table,
           token_mask, relative_ids, horizontal_ids, vertical_ids, cotangent, NP=8, Z=4):
    c=Cfg()
    pages_here,sl,D=hidden.shape
    S=relative_ids.shape[1]
    c.R=S//2; c.S=S; c.SP=-(-S//128)*128; c.Z=Z; c.H=relative_table.shape[1]; c.D=D
    L=qkv_weight.shape[2]; c.HD=L//c.H; c.FZ=up_weight.shape[1]
    c.B1=relative_table.shape[0]; c.B2=horizontal_table.shape[0]
    g=lax.axis_index("pages"); z=lax.axis_index("heads"); k=g%2
    pairs=[[2*i,2*i+1] for i in range(NP//2)]
    swap=[(i,i^1) for i in range(NP)]
    def to_page(x):
        x=lax.all_gather(x,"pages",axis=0,tiled=True,axis_index_groups=pairs)
        return lax.all_to_all(x,"heads",split_axis=0,concat_axis=0,tiled=True).reshape(S,D)
    def from_page(x):
        x=lax.all_gather(x,"pages",axis=0,tiled=True,axis_index_groups=pairs).reshape(Z,sl,D)
        x=lax.all_to_all(x,"heads",split_axis=0,concat_axis=0,tiled=True)
        return lax.dynamic_slice_in_dim(x,k*pages_here,pages_here,0)
    xf=jnp.zeros((c.SP,D),bf).at[:S].set(to_page(hidden))
    ct=lax.dynamic_slice_in_dim(to_page(cotangent),k*c.R,c.R,0)
    owner=k==z//2
    def own_rows(x):
        page=lax.dynamic_index_in_dim(x,z%2,0,keepdims=False)
        mine=lax.dynamic_slice_in_dim(page,k*c.R,c.R,0)
        other=lax.ppermute(lax.dynamic_slice_in_dim(page,(1-k)*c.R,c.R,0),"pages",swap)
        return jnp.where(owner,mine,other)
    ids=[own_rows(x) for x in (relative_ids,horizontal_ids,vertical_ids)]
    mrow=lax.dynamic_index_in_dim(token_mask,z%2,0,keepdims=True)
    mrow=jnp.where(owner,mrow,lax.ppermute(mrow,"pages",swap)).astype(f32)
    mask=jnp.zeros((1,c.SP),f32).at[:,:S].set(mrow)
    wloc=jnp.stack([jnp.concatenate([qkv_weight.transpose(1,2,0).reshape(3*L,D),out_weight],0),up_weight,down_weight])
    e=D//8
    wl=lax.dynamic_slice_in_dim(wloc,(g%8)*e,e,1)
    wl=lax.all_gather(wl,"heads",axis=0)
    wl=lax.all_gather(wl,"pages",axis=0,axis_index_groups=[[8*i+j for j in range(8)] for i in range(NP//8)])
    W=wl.transpose(2,1,0,3,4).reshape(3,Z,D,D)
    qvb=lax.all_gather(qv_bias.astype(f32).reshape(1,2*L),"heads",axis=0,tiled=True)
    qvb=jnp.zeros((Z,8,2*L),f32).at[:,0].set(qvb)
    ub=lax.all_gather(up_bias.astype(f32)[None],"heads",axis=0,tiled=True)
    ub=jnp.zeros((Z,8,c.FZ),f32).at[:,0].set(ub)
    tb=jnp.zeros((3,c.H,128),f32)
    for t,x in enumerate((relative_table,horizontal_table,vertical_table)):
        tb=tb.at[t,:,:x.shape[0]].set(x.T.astype(f32))
    tb=lax.all_gather(tb,"heads",axis=1,tiled=True)
    tab=jnp.zeros((3,16,128),f32).at[:,:Z*c.H].set(tb)
    vec=jnp.stack([out_bias,first_gain,first_shift,down_bias,second_gain,second_shift,out_bias,out_bias]).astype(f32)
    kern=lambda *r: compute_kernel(c,lambda: pl.multiple_of((lax.axis_index("pages")%2)*c.R,16),*r)
    out,dh,ga,gu,gd,sm,tg=pl.pallas_call(kern,out_shape=outs(c),scratch_shapes=scratch(c),in_specs=specs()[0],out_specs=specs()[1],
        compiler_params=pltpu.CompilerParams(vmem_limit_bytes=67043328))(xf,ct,*ids,mask,W[0],W[1],W[2],qvb,ub,tab,vec)
    mine=lax.dynamic_slice_in_dim(dh,k*c.R,c.R,0)
    other=lax.ppermute(lax.dynamic_slice_in_dim(dh,(1-k)*c.R,c.R,0).astype(bf),"pages",swap)
    gh=from_page((mine+other.astype(f32)).astype(bf))
    o=from_page(out)
    G=jnp.stack([ga,gu,gd]).reshape(3,Z,NP,D//NP,D).transpose(2,1,0,3,4)
    G=lax.psum_scatter(G,"pages",scatter_dimension=0,tiled=False)
    G=lax.psum_scatter(G,"heads",scatter_dimension=0,tiled=False)
    G=lax.all_gather(G,"pages",axis=1,tiled=True).astype(f32)
    gq=G[0,:3*L].reshape(3,L,D).transpose(2,0,1)
    sm,tg=lax.psum((sm,tg),("pages","heads"))
    pick=lambda r0: lax.dynamic_index_in_dim(sm[r0:r0+8*Z].reshape(Z,8,D)[:,0],z,0,keepdims=False)
    gqv=jnp.stack([pick(40)[:L],pick(40+8*Z)[:L]])
    tl=lax.dynamic_slice_in_dim(tg,z*c.H,c.H,0).T
    return (o,gh,gq,gqv,G[0,3*L:],sm[0],sm[1],sm[2],G[1],pick(8),G[2],sm[3],sm[4],sm[5],tl[:c.B1],tl[c.B1:c.B1+c.B2],tl[c.B1+c.B2:])

def solution(mesh):
    in_specs = (
        P("pages", "heads", None),
        P(None, None, "heads"),
        P(None, "heads"),
        P("heads", None),
        P(),
        P(),
        P(),
        P(None, "heads"),
        P("heads"),
        P("heads", None),
        P(),
        P(),
        P(),
        P(None, "heads"),
        P(None, "heads"),
        P(None, "heads"),
        P("pages", None),
        P("pages", None, None),
        P("pages", None, None),
        P("pages", None, None),
        P("pages", "heads", None),
    )
    out_specs = (
        P("pages", "heads", None),
        P("pages", "heads", None),
        P(None, None, "heads"),
        P(None, "heads"),
        P("heads", None),
        P(),
        P(),
        P(),
        P(None, "heads"),
        P("heads"),
        P("heads", None),
        P(),
        P(),
        P(),
        P(None, "heads"),
        P(None, "heads"),
        P(None, "heads"),
    )
    f = lambda *a: shards(*a, NP=mesh.shape['pages'], Z=mesh.shape['heads'])
    return jax.shard_map(f, mesh=mesh, in_specs=in_specs, out_specs=out_specs, check_vma=False)
```
